512 devices in a mesh: tp: 8 (over y), vocab: 64 (over x, z, core).
Axes of the slice: x: 4, y: 8, z: 8, core: 2. Of those that a mesh axis runs over, the one named last changes fastest.
Arguments:
- partials: float32 [8, 1024, 8192], P('tp', 'vocab'), may hold values from -2.5 to 2.5
- residual: bfloat16 [1024, 8192], P('vocab', 'tp'), may hold values from -16 to 16
- norm_gain: float32 [8192], P('tp'), may hold values from 0.5 to 1.5
- head_weight: bfloat16 [8192, 98304], P('tp', 'vocab'), may hold values from -8 to 8
- owners: int32 [1024], P('tp'), may hold values from 0 to 63, as said below
- allowed: int32 [1024, 256], P('tp'), may hold values from 0 to 768, as said below
- counts: int32 [1024], P('tp'), may hold values from 1 to 256, as said below
Outputs:
- allowed_logprobs: float32 [2048, 256, 128], P(('tp', 'vocab'))
The draws below stay inside these ranges and needn't reach their ends.
Inputs may be any that keep to these rules, and one draw needn't show every extreme that they name: `owners`: within each group of 128 consecutive rows no owner has more than 4 rows, and one owner has exactly 4. `allowed`: block b holds vocabulary ids 128 * b to 128 * b + 127. The first counts[r] entries of a row are distinct and ascending, the rest equal 768; at most 4 of a row's blocks lie among blocks 12 * v to 12 * v + 11 for any v, and in each group of rows the rows of one owner reach 4 for every v. `counts`: each group of 128 consecutive rows has a row with 256.
All inputs are finite; a program needn't handle non-finite values.
Results may differ from the reference program's by a relative error of at most 0.00032.
Values sent between devices are 32-bit elements; how exact they have to be, the bound alone decides.
A program may use at most 64 MiB of HBM per device.

```python
import math
import jax
import jax.numpy as jnp
from jax import lax

D = 8192
BLOCK = 128
VBLK_DEV = 12
KMAX = 4
ROW_DEV = 2
ROWS = 1024
VOCAB = 98304
NBLK = 768
MAXB = 256
CAP = 4
N_TP = 8
N_VOCAB = 64


def common_sign(key):
    flips = jax.random.bernoulli(jax.random.fold_in(key, 5), 0.5, (D,))
    return jnp.where(flips, 1.0, -1.0).astype(jnp.float32)


def request_plan(key):
    plan_key = jax.random.fold_in(key, 11)
    block_rows = N_VOCAB * ROW_DEV
    slots_all = N_VOCAB * CAP

    def one_block(block_key):
        subkeys = jax.random.split(block_key, 5)
        busiest = jax.random.randint(subkeys[0], (), 0, N_VOCAB)
        slot_ids = jnp.arange(slots_all, dtype=jnp.int32)
        scores = jax.random.permutation(subkeys[1], slots_all).astype(jnp.int32)
        scores = jnp.where(slot_ids // CAP == busiest, scores - slots_all, scores)
        chosen = jnp.argsort(scores)[:block_rows]
        chosen = jax.random.permutation(subkeys[2], chosen)
        owner_ids = (chosen // CAP).astype(jnp.int32)
        run_sizes = jax.random.randint(subkeys[3], (block_rows, N_VOCAB), 0, KMAX + 1)
        row_ids = jnp.arange(block_rows, dtype=jnp.int32)
        slice_ids = jnp.arange(N_VOCAB, dtype=jnp.int32)
        forced = slice_ids[None, :] == (row_ids % N_VOCAB)[:, None]
        run_sizes = jnp.where(forced, jnp.maximum(run_sizes, 1), run_sizes)
        run_sizes = jnp.where((owner_ids == busiest)[:, None], KMAX, run_sizes)
        ordered = jnp.broadcast_to(jnp.arange(VBLK_DEV, dtype=jnp.int32), (block_rows, N_VOCAB, VBLK_DEV))
        shuffled = jax.random.permutation(subkeys[4], ordered, axis=2, independent=True)
        taken_mask = (shuffled < run_sizes[:, :, None]).reshape(block_rows, NBLK)
        position = jnp.cumsum(taken_mask.astype(jnp.int32), axis=1) - 1
        position = jnp.where(taken_mask, position, MAXB)
        block_ids = jnp.broadcast_to(jnp.arange(NBLK, dtype=jnp.int32), (block_rows, NBLK))
        block_lists = jnp.full((block_rows, MAXB), NBLK, jnp.int32)
        block_lists = block_lists.at[row_ids[:, None], position].set(block_ids, mode='drop')
        totals = jnp.sum(taken_mask.astype(jnp.int32), axis=1)
        return (owner_ids, block_lists, totals)
    block_keys = jax.random.split(plan_key, N_TP)
    owner_ids, block_lists, totals = jax.vmap(one_block)(block_keys)
    return (owner_ids.reshape(ROWS), block_lists.reshape(ROWS, MAXB), totals.reshape(ROWS))


def draw_owners(key, part):
    return request_plan(key)[0]


def draw_allowed(key, part):
    return request_plan(key)[1]


def draw_counts(key, part):
    return request_plan(key)[2]


def draw_residual(key, part):
    sign = common_sign(key)
    subkeys = jax.random.split(jax.random.fold_in(key, 21), 5)
    ramp = 0.4 + 1.4 * jnp.arange(D, dtype=jnp.float32) / D
    values = jnp.clip(jax.random.normal(subkeys[0], (ROWS, D)), -4.0, 4.0) * ramp[None, :]
    aligned = jax.random.uniform(subkeys[3], (ROWS, 1)) < 0.04
    picked_row = jax.random.randint(subkeys[4], (), 0, ROWS)
    aligned = aligned | (jnp.arange(ROWS)[:, None] == picked_row)
    values = jnp.where(aligned, 16.0 * sign[None, :], values)
    return values.astype(jnp.bfloat16)


def draw_head_weight(key, part):
    sign = common_sign(key)
    subkeys = jax.random.split(jax.random.fold_in(key, 31), 6)
    noise = jnp.clip(jax.random.normal(subkeys[0], (D, VOCAB)), -6.0, 6.0)
    root = math.sqrt(D)
    ramp = 3.0 + 0.35 * jnp.arange(VOCAB, dtype=jnp.float32) / VOCAB
    weight = noise * ramp[None, :] / root
    pairs = VOCAB // 2
    paired = jax.random.uniform(subkeys[2], (pairs,)) < 0.004
    paired = paired | (jnp.arange(pairs) == jax.random.randint(subkeys[3], (), 0, pairs))
    strength = jax.random.uniform(subkeys[4], (pairs,), minval=120.0, maxval=320.0)
    spacing = jax.random.uniform(subkeys[5], (pairs,), minval=1.0, maxval=3.0)
    second = jnp.stack([jnp.zeros((pairs,), jnp.float32), spacing], axis=1).reshape(VOCAB)
    coefficient = jnp.repeat(strength, 2) + second
    weight = jnp.where(jnp.repeat(paired, 2)[None, :], sign[:, None] * coefficient[None, :] / D, weight)
    return weight.astype(jnp.bfloat16)


def with_spikes(entries, rng, source, target, shards_of, factor):
    def block_of(dim):
        return (jnp.arange(entries.shape[dim]) // (entries.shape[dim] // shards_of)).reshape((-1,) + (1,) * (entries.ndim - 1 - dim))

    near = jax.random.permutation(rng, shards_of)[block_of(target)]
    other_side = (block_of(target) + shards_of // 2) % shards_of
    return jnp.where((block_of(source) == near) | (block_of(source) == other_side), factor * entries, entries)


def block_levels(stream_key, extent, pieces, low, high):
    level = 1.0
    for axis_at, shards_of in pieces:
        heights = jax.random.uniform(jax.random.fold_in(jax.random.fold_in(stream_key, 6), axis_at), (shards_of,), jnp.float32, low / len(pieces), high / len(pieces))
        level = level * jnp.repeat(jnp.exp(heights), extent[axis_at] // shards_of).reshape((-1,) + (1,) * (len(extent) - 1 - axis_at))
    return level


def gaussian_with(key, dims, width, reach, shards, heavy, kind=jnp.bfloat16):
    array = width * jax.random.normal(key, dims, jnp.float32)
    if shards:
        array = array * block_levels(key, dims, shards, -0.22, 0.18)
    return jnp.clip(with_spikes(array, jax.random.fold_in(key, 3), *heavy), -reach, reach).astype(kind)


def setup_inputs(seed: int = 0) -> dict:
    key_list = jax.random.split(jax.random.key(seed), 8)
    partials = gaussian_with(key_list[0], (N_TP, ROWS, D), 0.35, 2.5, ((0, 8), (1, 64)), (0, 2, 8, 2.0), jnp.float32)
    residual = draw_residual(jax.random.fold_in(key_list[7], 71), 0)
    norm_gain = jnp.clip(1.0 + 0.1 * jax.random.normal(key_list[2], (D,), jnp.float32), 0.5, 1.5)
    head_weight = draw_head_weight(jax.random.fold_in(key_list[7], 71), 0)
    owners = draw_owners(jax.random.fold_in(key_list[7], 71), 0)
    allowed = draw_allowed(jax.random.fold_in(key_list[7], 71), 0)
    counts = draw_counts(jax.random.fold_in(key_list[7], 71), 0)
    return {"partials": partials, "residual": residual, "norm_gain": norm_gain, "head_weight": head_weight, "owners": owners, "allowed": allowed, "counts": counts}


EPSILON = 1e-05

def reference(partials, residual, norm_gain, head_weight, owners, allowed, counts):
    mixed = lax.optimization_barrier(jnp.sum(partials, axis=0)) + residual.astype(jnp.float32)
    sumsq = lax.optimization_barrier(jnp.sum(mixed * mixed, axis=1))
    scaled = (mixed * norm_gain).astype(jnp.bfloat16)
    raw_logits = jnp.dot(scaled, head_weight, preferred_element_type=jnp.float32)
    logits = raw_logits * lax.rsqrt(sumsq / D + EPSILON)[:, None]
    row_top = lax.optimization_barrier(jnp.max(logits, axis=1))
    row_total = lax.optimization_barrier(jnp.sum(jnp.exp(logits - row_top[:, None]), axis=1))
    logprob = logits - (row_top + jnp.log(row_total))[:, None]
    per_group = ROWS // N_TP
    row_order = jnp.arange(ROWS, dtype=jnp.int32)
    row_group = row_order // per_group
    same_owner = (owners[:, None] == owners[None, :]) & (row_group[:, None] == row_group[None, :]) & (row_order[:, None] < row_order[None, :])
    slot_rank = lax.optimization_barrier(jnp.sum(same_owner.astype(jnp.int32), axis=0))
    target_row = (row_group * N_VOCAB + owners) * CAP + slot_rank
    positions = jnp.arange(MAXB, dtype=jnp.int32)
    live_entry = positions[None, :] < counts[:, None]
    safe_ids = jnp.where(live_entry, allowed, 0).astype(jnp.int32)
    id_blocks = logprob.reshape(ROWS, NBLK, BLOCK)
    picked = jnp.take_along_axis(id_blocks, safe_ids[:, :, None], axis=1)
    picked = jnp.where(live_entry[:, :, None], picked, 0.0)
    placed = jnp.zeros((N_TP * N_VOCAB * CAP, MAXB, BLOCK), jnp.float32)
    return placed.at[target_row].set(picked)
```

```python
import jax
import jax.numpy as jnp
from jax import lax
from jax.sharding import PartitionSpec as P

EPSILON = 1e-05
BLOCK = 128
KMAX = 4


def slot_ranks(owners):
    row_order = jnp.arange(owners.shape[0], dtype=jnp.int32)
    same_owner = (owners[:, None] == owners[None, :]) & (row_order[:, None] < row_order[None, :])
    return jnp.sum(same_owner.astype(jnp.int32), axis=0)


def tail(raw_logits, sumsq, width, owners, allowed, counts):
    vocab_count = lax.axis_size("vocab")
    vocab_index = lax.axis_index("vocab")
    own_rows, columns = raw_logits.shape
    blocks_here = columns // BLOCK
    list_width = allowed.shape[1]
    per_owner = 2 * own_rows // vocab_count
    positions = jnp.arange(list_width, dtype=jnp.int32)

    slot_rank = slot_ranks(owners)
    mine = jnp.where(positions[None, :] < counts[:, None], allowed, -1) - vocab_index * blocks_here
    here = jnp.arange(blocks_here, dtype=jnp.int32)
    present = jnp.any(mine[:, None, :] == here[None, :, None], axis=2).astype(jnp.int32)
    place = jnp.sum(jnp.where(here[:, None] < here[None, :], present[:, :, None], 0), axis=1)
    place = jnp.where(present > 0, place, -1)
    target_row = owners * per_owner + slot_rank
    slots = jnp.arange(vocab_count * per_owner, dtype=jnp.int32)
    to_slot = (target_row[None, :] == slots[:, None]).astype(jnp.float32)

    slot_index = jnp.arange(per_owner, dtype=jnp.int32)[:, None]
    owned_slot = ((owners[None, :] == vocab_index) & (slot_rank[None, :] == slot_index)).astype(jnp.int32)
    slot_lists = jnp.sum(owned_slot[:, :, None] * allowed[None, :, :], axis=1)
    slot_counts = jnp.sum(owned_slot * counts[None, :], axis=1)
    live_entry = positions[None, :] < slot_counts[:, None]
    source = jnp.clip(slot_lists // blocks_here, 0, vocab_count - 1)
    rank = jnp.zeros_like(source)
    for back in range(1, KMAX):
        earlier = jnp.pad(source, ((0, 0), (back, 0)), constant_values=-1)[:, :list_width]
        rank = rank + (earlier == source).astype(jnp.int32)
    table_row = (source * per_owner + slot_index) * (KMAX + 1) + jnp.minimum(rank, KMAX - 1)
    table_row = jnp.where(live_entry, table_row, 0)

    logits = raw_logits * lax.rsqrt(sumsq / width + EPSILON)[:, None]
    row_top = jnp.max(logits, axis=1)
    row_total = jnp.sum(jnp.exp(logits - row_top[:, None]), axis=1)
    picked = []
    for k in range(KMAX):
        chosen = jnp.zeros((own_rows, BLOCK), jnp.float32)
        for b in range(blocks_here):
            block = logits[:, b * BLOCK : (b + 1) * BLOCK]
            chosen = jnp.where((place[:, b] == k)[:, None], block, chosen)
        picked.append(chosen)
    lane = jnp.arange(BLOCK, dtype=jnp.int32)[None, :]
    picked.append(jnp.where(lane == 0, row_top[:, None], jnp.where(lane == 1, row_total[:, None], 0.0)))
    payload = jnp.concatenate(picked, axis=1)
    outgoing = jnp.dot(
        to_slot, payload, precision=lax.Precision.HIGHEST, preferred_element_type=jnp.float32
    ).reshape(vocab_count, per_owner, (KMAX + 1) * BLOCK)
    incoming = lax.all_to_all(outgoing, "vocab", split_axis=0, concat_axis=0, tiled=True)
    tops = incoming[:, :, KMAX * BLOCK]
    totals = incoming[:, :, KMAX * BLOCK + 1]
    big_top = jnp.max(tops, axis=0)
    big_total = jnp.sum(totals * jnp.exp(tops - big_top[None, :]), axis=0)
    shift = big_top + jnp.log(big_total)
    received = incoming.reshape(vocab_count * per_owner * (KMAX + 1), BLOCK)
    gathered = jnp.take(received, table_row, axis=0)
    return jnp.where(live_entry[:, :, None], gathered - shift[:, None, None], 0.0)


def body(partials, residual, norm_gain, head_weight, owners, allowed, counts):
    summed = lax.psum_scatter(partials, "tp", scatter_dimension=2, tiled=True)[0]
    hidden_rows = summed + residual.astype(jnp.float32)
    every_row = lax.all_gather(hidden_rows, "vocab", axis=0, tiled=True)
    square_part = jnp.sum(every_row * every_row, axis=1)
    scaled = (every_row * norm_gain).astype(jnp.bfloat16)
    head_terms = jnp.dot(scaled, head_weight, preferred_element_type=jnp.float32)
    raw_logits = lax.psum_scatter(head_terms, "tp", scatter_dimension=0, tiled=True)
    sumsq = lax.psum_scatter(square_part, "tp", scatter_dimension=0, tiled=True)
    width = head_weight.shape[0] * lax.axis_size("tp")
    return tail(raw_logits, sumsq, width, owners, allowed, counts)


def solution(mesh):
    placed = (
        P("tp", "vocab", None),
        P("vocab", "tp"),
        P("tp"),
        P("tp", "vocab"),
        P("tp"),
        P("tp", None),
        P("tp"),
    )
    return jax.shard_map(
        body, mesh=mesh, in_specs=placed, out_specs=P(("tp", "vocab"), None, None), check_vma=False
    )
```

```python
import jax
import jax.numpy as jnp
from jax import lax
from jax.experimental import pallas as pl
from jax.experimental.pallas import tpu as pltpu
from jax.sharding import PartitionSpec as P

EPSILON = 1e-05
BLOCK = 128
KMAX = 4


def slot_ranks(owners):
    row_order = jnp.arange(owners.shape[0], dtype=jnp.int32)
    same_owner = (owners[:, None] == owners[None, :]) & (row_order[:, None] < row_order[None, :])
    return jnp.sum(same_owner.astype(jnp.int32), axis=0)


def tail(raw_logits, sumsq, width, owners, allowed, counts):
    vocab_count = lax.axis_size("vocab")
    vocab_index = lax.axis_index("vocab")
    own_rows, columns = raw_logits.shape
    blocks_here = columns // BLOCK
    list_width = allowed.shape[1]
    per_owner = 2 * own_rows // vocab_count
    positions = jnp.arange(list_width, dtype=jnp.int32)

    slot_rank = slot_ranks(owners)
    mine = jnp.where(positions[None, :] < counts[:, None], allowed, -1) - vocab_index * blocks_here
    here = jnp.arange(blocks_here, dtype=jnp.int32)
    present = jnp.any(mine[:, None, :] == here[None, :, None], axis=2).astype(jnp.int32)
    place = jnp.sum(jnp.where(here[:, None] < here[None, :], present[:, :, None], 0), axis=1)
    place = jnp.where(present > 0, place, -1)
    target_row = owners * per_owner + slot_rank
    slots = jnp.arange(vocab_count * per_owner, dtype=jnp.int32)
    to_slot = (target_row[None, :] == slots[:, None]).astype(jnp.float32)

    slot_index = jnp.arange(per_owner, dtype=jnp.int32)[:, None]
    owned_slot = ((owners[None, :] == vocab_index) & (slot_rank[None, :] == slot_index)).astype(jnp.int32)
    slot_lists = jnp.sum(owned_slot[:, :, None] * allowed[None, :, :], axis=1)
    slot_counts = jnp.sum(owned_slot * counts[None, :], axis=1)
    live_entry = positions[None, :] < slot_counts[:, None]
    source = jnp.clip(slot_lists // blocks_here, 0, vocab_count - 1)
    rank = jnp.zeros_like(source)
    for back in range(1, KMAX):
        earlier = jnp.pad(source, ((0, 0), (back, 0)), constant_values=-1)[:, :list_width]
        rank = rank + (earlier == source).astype(jnp.int32)
    table_row = (source * per_owner + slot_index) * (KMAX + 1) + jnp.minimum(rank, KMAX - 1)
    table_row = jnp.where(live_entry, table_row, 0)

    logits = raw_logits * lax.rsqrt(sumsq / width + EPSILON)[:, None]
    row_top = jnp.max(logits, axis=1)
    row_total = jnp.sum(jnp.exp(logits - row_top[:, None]), axis=1)
    picked = []
    for k in range(KMAX):
        chosen = jnp.zeros((own_rows, BLOCK), jnp.float32)
        for b in range(blocks_here):
            block = logits[:, b * BLOCK : (b + 1) * BLOCK]
            chosen = jnp.where((place[:, b] == k)[:, None], block, chosen)
        picked.append(chosen)
    lane = jnp.arange(BLOCK, dtype=jnp.int32)[None, :]
    picked.append(jnp.where(lane == 0, row_top[:, None], jnp.where(lane == 1, row_total[:, None], 0.0)))
    payload = jnp.concatenate(picked, axis=1)
    outgoing = jnp.dot(
        to_slot, payload, precision=lax.Precision.HIGHEST, preferred_element_type=jnp.float32
    ).reshape(vocab_count, per_owner, (KMAX + 1) * BLOCK)
    incoming = lax.all_to_all(outgoing, "vocab", split_axis=0, concat_axis=0, tiled=True)
    tops = incoming[:, :, KMAX * BLOCK]
    totals = incoming[:, :, KMAX * BLOCK + 1]
    big_top = jnp.max(tops, axis=0)
    big_total = jnp.sum(totals * jnp.exp(tops - big_top[None, :]), axis=0)
    shift = big_top + jnp.log(big_total)
    received = incoming.reshape(vocab_count * per_owner * (KMAX + 1), BLOCK)
    gathered = jnp.take(received, table_row, axis=0)
    return jnp.where(live_entry[:, :, None], gathered - shift[:, None, None], 0.0)


N_Y, N_X, N_Z = 8, 4, 8
SUBS = 3


def head_kernel(
    part_ref, res_ref, gain_ref, w_hbm, raw_ref, sq_ref,
    w, rs_in, rows, scaled, col, sq_part, sq_in, ring, term,
    w_sem, rs_s, rs_r, ag_s, ag_r, ring_s, ring_r, sq_s, sq_r,
):
    y = lax.axis_index("tp")
    v = lax.axis_index("vocab")
    core = lax.rem(v, 2)
    z = lax.rem(lax.div(v, 2), N_Z)
    x = lax.div(v, 2 * N_Z)
    turn = 1 - 2 * core
    local_rows, share = res_ref.shape
    half = share // 2
    group = N_Y * local_rows

    def at_x(q):
        return lax.rem(x - turn * q + N_X, N_X)

    def at_z(p):
        return lax.rem(z - turn * p + N_Z, N_Z)

    def device(p, q, c):
        return (y, (at_x(q) * N_Z + at_z(p)) * 2 + c)

    def along_tp(d):
        return (lax.rem(y + d + N_Y, N_Y), v)

    weight_copy = pltpu.make_async_copy(w_hbm, w, w_sem)
    weight_copy.start()

    peers = [along_tp(d) for d in range(1, N_Y)]
    peers += [device(-1, 0, core), device(1, 0, core), device(0, -1, core), device(0, 1, core)]
    peers += [device(0, 0, 1 - core)]
    barrier = pltpu.get_barrier_semaphore()
    for peer in peers:
        pl.semaphore_signal(barrier, inc=1, device_id=peer, device_id_type=pl.DeviceIdType.MESH)
    pl.semaphore_wait(barrier, len(peers))

    def remote(src, dst, send_sem, recv_sem, peer):
        return pltpu.make_async_remote_copy(
            src_ref=src, dst_ref=dst, send_sem=send_sem, recv_sem=recv_sem,
            device_id=peer, device_id_type=pl.DeviceIdType.MESH,
        )

    first = []
    for d in (1, 7, 2, 6, 3, 5, 4):
        to = lax.rem(y + d, N_Y)
        source = part_ref.at[0, :, pl.ds(pl.multiple_of(to * share, share), share)]
        copy = remote(source, rs_in.at[d - 1], rs_s.at[d - 1], rs_r.at[d - 1], along_tp(d))
        copy.start()
        first.append(copy)
    mixed = part_ref[0, :, pl.ds(pl.multiple_of(y * share, share), share)]
    mixed = mixed + res_ref[...].astype(jnp.float32)
    for copy in first:
        copy.wait_recv()
    for d in range(1, N_Y):
        mixed = mixed + rs_in[d - 1]
    own = x * N_Z + z
    rows[0, core, own] = mixed[:, :half]
    rows[1, core, own] = mixed[:, half:]

    limits = {"z": (N_Z // 2, N_Z // 2 - 1), "x": (N_X // 2, N_X // 2 - 1)}
    places = [
        (h, p, q)
        for h in range(2)
        for p in range(-limits["z"][1], limits["z"][0] + 1)
        for q in range(-limits["x"][1], limits["x"][0] + 1)
    ]
    ids = {place: i for i, place in enumerate(places)}
    sent = []

    def held(h, p, q):
        return rows.at[h, core, at_x(q) * N_Z + at_z(p)]

    def pass_on(h, p, q, new_p, new_q):
        peer = device(p - new_p, q - new_q, core)
        i = ids[(h, new_p, new_q)]
        copy = remote(held(h, p, q), held(h, p, q), ag_s.at[0, i], ag_r.at[0, i], peer)
        copy.start()
        sent.append(copy)

    def to_sibling(h, p, q):
        i = ids[(h, p, q)]
        copy = remote(
            held(h, p, q), held(h, p, q), ag_s.at[1, i], ag_r.at[1, i], device(0, 0, 1 - core)
        )
        copy.start()
        sent.append(copy)

    def along_z(h, p, q):
        if 0 <= p < limits["z"][0]:
            pass_on(h, p, q, p + 1, q)
        if -limits["z"][1] < p <= 0:
            pass_on(h, p, q, p - 1, q)

    def along_x(h, p, q):
        if 0 <= q < limits["x"][0]:
            pass_on(h, p, q, p, q + 1)
        if -limits["x"][1] < q <= 0:
            pass_on(h, p, q, p, q - 1)

    def arrived(h, p, q):
        if h == 0:
            if q == 0:
                along_z(h, p, q)
            along_x(h, p, q)
        else:
            if p == 0:
                along_x(h, p, q)
            along_z(h, p, q)
        to_sibling(h, p, q)

    def order(place):
        h, p, q = place
        main, other = (p, q) if h == 0 else (q, p)
        return (abs(p) + abs(q), abs(other), h, main)

    for h, p, q in sorted(places, key=order):
        if (p, q) != (0, 0):
            i = ids[(h, p, q)]
            block = held(h, p, q)
            remote(block, block, ag_s.at[0, i], ag_r.at[0, i], device(0, 0, 1 - core)).wait_recv()
        arrived(h, p, q)
    for h, p, q in sorted(places, key=order):
        i = ids[(h, p, q)]
        block = rows.at[h, 1 - core, at_x(-q) * N_Z + at_z(-p)]
        remote(block, block, ag_s.at[1, i], ag_r.at[1, i], device(0, 0, 1 - core)).wait_recv()

    def prepare(g):
        for b in range(N_Y):
            at = lax.div(g * N_Y, 2) + b // 2
            low = rows[0, b % 2, at]
            high = rows[1, b % 2, at]
            start = pl.multiple_of(g * group + b * local_rows, local_rows)
            scaled[pl.ds(start, local_rows), :half] = (low * gain_ref[:, :half]).astype(jnp.bfloat16)
            scaled[pl.ds(start, local_rows), half:] = (high * gain_ref[:, half:]).astype(jnp.bfloat16)
            squares = jnp.sum(low * low + high * high, axis=1, keepdims=True)
            col[b * local_rows : (b + 1) * local_rows, :] = jnp.broadcast_to(
                squares, (local_rows, BLOCK)
            )
        sq_part[g] = jnp.transpose(col[...])[:8]

    width = ring.shape[-1]

    def own_term(g, way, j):
        left = scaled[pl.ds(pl.multiple_of(g * group, group), group), :]
        start = (way * SUBS + j) * width
        return jnp.dot(left, w[:, start : start + width], preferred_element_type=jnp.float32)

    def group_at(way, s):
        return lax.rem(y + N_Y - 1 - s, N_Y) if way == 0 else lax.rem(y + 1 + s, N_Y)

    def hop(way, s, j):
        return remote(
            ring.at[way, s, j], ring.at[way, s + 1, j], ring_s.at[way, s, j], ring_r.at[way, s, j],
            along_tp(1 if way == 0 else -1),
        )

    weight_copy.wait()
    for way in range(2):
        prepare(group_at(way, 0))
        for j in range(SUBS):
            ring[way, 0, j] = own_term(group_at(way, 0), way, j)
            hop(way, 0, j).start()

    @pl.loop(2, N_Y + 1)
    def _(k):
        @pl.when(k != N_Y - 1)
        def _():
            prepare(lax.rem(y + k, N_Y))

    squares_out = []
    for d in range(1, N_Y):
        to = lax.rem(y + d, N_Y)
        copy = remote(sq_part.at[to], sq_in.at[d - 1], sq_s.at[d - 1], sq_r.at[d - 1], along_tp(d))
        copy.start()
        squares_out.append(copy)

    @pl.loop(1, N_Y - 1)
    def _(s):
        for way in range(2):
            for j in range(SUBS):
                term[way, j] = own_term(group_at(way, s), way, j)
        for j in range(SUBS):
            for way in range(2):
                hop(way, s - 1, j).wait_recv()
                ring[way, s, j] = ring[way, s, j] + term[way, j]
                hop(way, s, j).start()

    for way in range(2):
        for j in range(SUBS):
            term[way, j] = own_term(y, way, j)
    for copy in squares_out:
        copy.wait_recv()
    total = sq_part[y]
    for d in range(1, N_Y):
        total = total + sq_in[d - 1]
    sq_ref[...] = total
    for j in range(SUBS):
        for way in range(2):
            hop(way, N_Y - 2, j).wait_recv()
            start = (way * SUBS + j) * width
            raw_ref[:, start : start + width] = ring[way, N_Y - 1, j] + term[way, j]

    for copy in first + sent + squares_out:
        copy.wait_send()

    @pl.loop(0, N_Y - 1)
    def _(s):
        for way in range(2):
            for j in range(SUBS):
                hop(way, s, j).wait_send()


def head(partials, residual, norm_gain, head_weight):
    local_rows, share = residual.shape
    columns = head_weight.shape[1]
    group = N_Y * local_rows
    chips = N_X * N_Z
    width = columns // (2 * SUBS)
    dma = pltpu.SemaphoreType.DMA
    f32 = jnp.float32
    vmem = pl.BlockSpec(memory_space=pltpu.VMEM)
    raw, squares = pl.pallas_call(
        head_kernel,
        out_shape=[
            jax.ShapeDtypeStruct((group, columns), f32),
            jax.ShapeDtypeStruct((8, BLOCK), f32),
        ],
        in_specs=[vmem, vmem, vmem, pl.BlockSpec(memory_space=pl.ANY)],
        out_specs=[vmem, vmem],
        scratch_shapes=[
            pltpu.VMEM((share, columns), jnp.bfloat16),
            pltpu.VMEM((N_Y - 1, local_rows, share), f32),
            pltpu.VMEM((2, 2, chips, local_rows, share // 2), f32),
            pltpu.VMEM((2 * chips * local_rows, share), jnp.bfloat16),
            pltpu.VMEM((group, BLOCK), f32),
            pltpu.VMEM((N_Y, 8, BLOCK), f32),
            pltpu.VMEM((N_Y - 1, 8, BLOCK), f32),
            pltpu.VMEM((2, N_Y, SUBS, group, width), f32),
            pltpu.VMEM((2, SUBS, group, width), f32),
            dma,
            dma((N_Y - 1,)),
            dma((N_Y - 1,)),
            dma((2, 2 * chips)),
            dma((2, 2 * chips)),
            dma((2, N_Y - 1, SUBS)),
            dma((2, N_Y - 1, SUBS)),
            dma((N_Y - 1,)),
            dma((N_Y - 1,)),
        ],
        compiler_params=pltpu.CompilerParams(
            collective_id=0, has_side_effects=True, vmem_limit_bytes=48 << 20
        ),
    )(partials, residual, norm_gain.reshape(1, share), head_weight)
    return raw, squares[0]


def body(partials, residual, norm_gain, head_weight, owners, allowed, counts):
    raw_logits, sumsq = head(partials, residual, norm_gain, head_weight)
    width = head_weight.shape[0] * lax.axis_size("tp")
    return tail(raw_logits, sumsq, width, owners, allowed, counts)


def solution(mesh):
    placed = (
        P("tp", "vocab", None),
        P("vocab", "tp"),
        P("tp"),
        P("tp", "vocab"),
        P("tp"),
        P("tp", None),
        P("tp"),
    )
    return jax.shard_map(
        body, mesh=mesh, in_specs=placed, out_specs=P(("tp", "vocab"), None, None), check_vma=False
    )
```

```python
import jax
import jax.numpy as jnp
from jax import lax
from jax.experimental import pallas as pl
from jax.experimental.pallas import tpu as pltpu
from jax.sharding import PartitionSpec as P

EPSILON = 1e-05
BLOCK = 128
KMAX = 4


def slot_ranks(owners):
    row_order = jnp.arange(owners.shape[0], dtype=jnp.int32)
    same_owner = (owners[:, None] == owners[None, :]) & (row_order[:, None] < row_order[None, :])
    return jnp.sum(same_owner.astype(jnp.int32), axis=0)


def tail(raw_logits, sumsq, width, owners, allowed, counts):
    vocab_count = lax.axis_size("vocab")
    vocab_index = lax.axis_index("vocab")
    own_rows, columns = raw_logits.shape
    blocks_here = columns // BLOCK
    list_width = allowed.shape[1]
    per_owner = 2 * own_rows // vocab_count
    positions = jnp.arange(list_width, dtype=jnp.int32)

    slot_rank = slot_ranks(owners)
    mine = jnp.where(positions[None, :] < counts[:, None], allowed, -1) - vocab_index * blocks_here
    here = jnp.arange(blocks_here, dtype=jnp.int32)
    present = jnp.any(mine[:, None, :] == here[None, :, None], axis=2).astype(jnp.int32)
    place = jnp.sum(jnp.where(here[:, None] < here[None, :], present[:, :, None], 0), axis=1)
    place = jnp.where(present > 0, place, -1)
    target_row = owners * per_owner + slot_rank
    slots = jnp.arange(vocab_count * per_owner, dtype=jnp.int32)
    to_slot = (target_row[None, :] == slots[:, None]).astype(jnp.float32)

    slot_index = jnp.arange(per_owner, dtype=jnp.int32)[:, None]
    owned_slot = ((owners[None, :] == vocab_index) & (slot_rank[None, :] == slot_index)).astype(jnp.int32)
    slot_lists = jnp.sum(owned_slot[:, :, None] * allowed[None, :, :], axis=1)
    slot_counts = jnp.sum(owned_slot * counts[None, :], axis=1)
    live_entry = positions[None, :] < slot_counts[:, None]
    source = jnp.clip(slot_lists // blocks_here, 0, vocab_count - 1)
    rank = jnp.zeros_like(source)
    for back in range(1, KMAX):
        earlier = jnp.pad(source, ((0, 0), (back, 0)), constant_values=-1)[:, :list_width]
        rank = rank + (earlier == source).astype(jnp.int32)
    table_row = (source * per_owner + slot_index) * (KMAX + 1) + jnp.minimum(rank, KMAX - 1)
    table_row = jnp.where(live_entry, table_row, 0)

    logits = raw_logits * lax.rsqrt(sumsq / width + EPSILON)[:, None]
    row_top = jnp.max(logits, axis=1)
    row_total = jnp.sum(jnp.exp(logits - row_top[:, None]), axis=1)
    picked = []
    for k in range(KMAX):
        chosen = jnp.zeros((own_rows, BLOCK), jnp.float32)
        for b in range(blocks_here):
            block = logits[:, b * BLOCK : (b + 1) * BLOCK]
            chosen = jnp.where((place[:, b] == k)[:, None], block, chosen)
        picked.append(chosen)
    lane = jnp.arange(BLOCK, dtype=jnp.int32)[None, :]
    picked.append(jnp.where(lane == 0, row_top[:, None], jnp.where(lane == 1, row_total[:, None], 0.0)))
    payload = jnp.concatenate(picked, axis=1)
    outgoing = jnp.dot(
        to_slot, payload, precision=lax.Precision.HIGHEST, preferred_element_type=jnp.float32
    ).reshape(vocab_count, per_owner, (KMAX + 1) * BLOCK)
    incoming = lax.all_to_all(outgoing, "vocab", split_axis=0, concat_axis=0, tiled=True)
    tops = incoming[:, :, KMAX * BLOCK]
    totals = incoming[:, :, KMAX * BLOCK + 1]
    big_top = jnp.max(tops, axis=0)
    big_total = jnp.sum(totals * jnp.exp(tops - big_top[None, :]), axis=0)
    shift = big_top + jnp.log(big_total)
    received = incoming.reshape(vocab_count * per_owner * (KMAX + 1), BLOCK)
    gathered = jnp.take(received, table_row, axis=0)
    return jnp.where(live_entry[:, :, None], gathered - shift[:, None, None], 0.0)


N_Y, N_X, N_Z = 8, 4, 8
SUBS = 3


def head_kernel(
    part_hbm, res_hbm, gain_hbm, w_hbm, raw_ref, sq_ref,
    w, part, res, gain, rs_in, rows, scaled, col, sq_part, sq_in, ring, term,
    in_sem, rs_s, rs_r, ag_s, ag_r, ring_s, ring_r, sq_s, sq_r,
):
    y = lax.axis_index("tp")
    v = lax.axis_index("vocab")
    core = lax.rem(v, 2)
    z = lax.rem(lax.div(v, 2), N_Z)
    x = lax.div(v, 2 * N_Z)
    turn = 1 - 2 * core
    local_rows, share = res.shape
    few = local_rows // 2
    group = N_Y * local_rows
    half = group // 2

    def at_x(q):
        return lax.rem(x - turn * q + N_X, N_X)

    def at_z(p):
        return lax.rem(z - turn * p + N_Z, N_Z)

    def device(p, q, c):
        return (y, (at_x(q) * N_Z + at_z(p)) * 2 + c)

    def along_tp(d):
        return (lax.rem(y + d + N_Y, N_Y), v)

    def columns_of(at):
        return pl.ds(pl.multiple_of(at * share, share), share)

    loads = [
        pltpu.make_async_copy(part_hbm.at[0, :, columns_of(y)], part, in_sem.at[0]),
        pltpu.make_async_copy(res_hbm, res, in_sem.at[1]),
        pltpu.make_async_copy(gain_hbm, gain, in_sem.at[2]),
        pltpu.make_async_copy(w_hbm, w, in_sem.at[3]),
    ]
    for load in loads:
        load.start()

    peers = [along_tp(d) for d in range(1, N_Y)]
    peers += [device(-1, 0, core), device(1, 0, core), device(0, -1, core), device(0, 1, core)]
    peers += [device(0, 0, 1 - core)]
    barrier = pltpu.get_barrier_semaphore()
    for peer in peers:
        pl.semaphore_signal(barrier, inc=1, device_id=peer, device_id_type=pl.DeviceIdType.MESH)
    pl.semaphore_wait(barrier, len(peers))

    def remote(src, dst, send_sem, recv_sem, peer):
        return pltpu.make_async_remote_copy(
            src_ref=src, dst_ref=dst, send_sem=send_sem, recv_sem=recv_sem,
            device_id=peer, device_id_type=pl.DeviceIdType.MESH,
        )

    first = {}
    for h in range(2):
        for d in (4, 1, 7, 2, 6, 3, 5):
            source = part_hbm.at[0, pl.ds(h * few, few), columns_of(lax.rem(y + d, N_Y))]
            copy = remote(
                source, rs_in.at[h, d - 1], rs_s.at[h, d - 1], rs_r.at[h, d - 1], along_tp(d)
            )
            copy.start()
            first[h, d] = copy
    for load in loads[:3]:
        load.wait()
    own = x * N_Z + z

    def mix(h):
        at = slice(h * few, (h + 1) * few)
        mixed = part[at] + res[...].astype(jnp.float32)[at]
        for d in range(1, N_Y):
            first[h, d].wait_recv()
        for d in range(1, N_Y):
            mixed = mixed + rs_in[h, d - 1]
        rows[h, core, own] = mixed

    limits = {"z": (N_Z // 2, N_Z // 2 - 1), "x": (N_X // 2, N_X // 2 - 1)}
    places = [
        (h, p, q)
        for h in range(2)
        for p in range(-limits["z"][1], limits["z"][0] + 1)
        for q in range(-limits["x"][1], limits["x"][0] + 1)
    ]
    ids = {place: i for i, place in enumerate(places)}
    sent = []

    def held(h, p, q):
        return rows.at[h, core, at_x(q) * N_Z + at_z(p)]

    def pass_on(h, p, q, new_p, new_q):
        peer = device(p - new_p, q - new_q, core)
        i = ids[(h, new_p, new_q)]
        copy = remote(held(h, p, q), held(h, p, q), ag_s.at[0, i], ag_r.at[0, i], peer)
        copy.start()
        sent.append(copy)

    def to_sibling(h, p, q):
        i = ids[(h, p, q)]
        copy = remote(
            held(h, p, q), held(h, p, q), ag_s.at[1, i], ag_r.at[1, i], device(0, 0, 1 - core)
        )
        copy.start()
        sent.append(copy)

    def along_z(h, p, q):
        if 0 <= p < limits["z"][0]:
            pass_on(h, p, q, p + 1, q)
        if -limits["z"][1] < p <= 0:
            pass_on(h, p, q, p - 1, q)

    def along_x(h, p, q):
        if 0 <= q < limits["x"][0]:
            pass_on(h, p, q, p, q + 1)
        if -limits["x"][1] < q <= 0:
            pass_on(h, p, q, p, q - 1)

    def arrived(h, p, q):
        if h == 0:
            if q == 0:
                along_z(h, p, q)
            along_x(h, p, q)
        else:
            if p == 0:
                along_x(h, p, q)
            along_z(h, p, q)
        to_sibling(h, p, q)

    def order(place):
        h, p, q = place
        main, other = (p, q) if h == 0 else (q, p)
        return (abs(p) + abs(q) + 2 * h, abs(other), h, main)

    def wait_siblings(h):
        for _, p, q in sorted((place for place in places if place[0] == h), key=order):
            i = ids[(h, p, q)]
            block = rows.at[h, 1 - core, at_x(-q) * N_Z + at_z(-p)]
            remote(block, block, ag_s.at[1, i], ag_r.at[1, i], device(0, 0, 1 - core)).wait_recv()

    def prepare(g, h):
        for b in range(N_Y // 2):
            at = lax.div(g * N_Y, 2) + b
            pair = jnp.concatenate([rows[h, 0, at], rows[h, 1, at]], axis=0) * gain[...]
            start = pl.multiple_of(g * group + h * half + b * local_rows, local_rows)
            scaled[pl.ds(start, local_rows), :] = pair.astype(jnp.bfloat16)

    def square(g):
        for b in range(N_Y):
            at = lax.div(g * N_Y, 2) + b // 2
            for h in range(2):
                block = rows[h, b % 2, at]
                squares = jnp.sum(block * block, axis=1, keepdims=True)
                start = b * local_rows + h * few
                col[start : start + few, :] = jnp.broadcast_to(squares, (few, BLOCK))
        sq_part[g] = jnp.transpose(col[...])[:8]

    width = ring.shape[-1]

    def own_term(g, way, j):
        left = scaled[pl.ds(pl.multiple_of(g * group, group), group), :]
        start = (way * SUBS + j) * width
        return jnp.dot(left, w[:, start : start + width], preferred_element_type=jnp.float32)

    def group_at(way, s):
        return lax.rem(y + N_Y - 1 - s, N_Y) if way == 0 else lax.rem(y + 1 + s, N_Y)

    def hop(way, s, j, h):
        at = pl.ds(h * half, half)
        return remote(
            ring.at[way, s, j, at], ring.at[way, s + 1, j, at],
            ring_s.at[way, s, j, h], ring_r.at[way, s, j, h],
            along_tp(1 if way == 0 else -1),
        )

    def begin(h):
        for way in range(2):
            g = group_at(way, 0)
            prepare(g, h)
            left = scaled[pl.ds(pl.multiple_of(g * group + h * half, half), half), :]
            for j in range(SUBS):
                start = (way * SUBS + j) * width
                ring[way, 0, j, h * half : (h + 1) * half] = jnp.dot(
                    left, w[:, start : start + width], preferred_element_type=jnp.float32
                )
                hop(way, 0, j, h).start()

    mix(0)
    waiting = sorted(places, key=order)
    for place in waiting:
        h, p, q = place
        if (p, q) == (0, 0):
            if h == 1:
                mix(1)
        else:
            i = ids[place]
            block = held(h, p, q)
            remote(block, block, ag_s.at[0, i], ag_r.at[0, i], device(0, 0, 1 - core)).wait_recv()
        arrived(h, p, q)
        if place == [other for other in waiting if other[0] == 0][-1]:
            wait_siblings(0)
            loads[3].wait()
            begin(0)
    wait_siblings(1)
    begin(1)

    @pl.loop(2, N_Y + 1)
    def _(k):
        @pl.when(k != N_Y - 1)
        def _():
            for h in range(2):
                prepare(lax.rem(y + k, N_Y), h)

    @pl.loop(0, N_Y)
    def _(g):
        square(g)

    squares_out = []
    for d in range(1, N_Y):
        to = lax.rem(y + d, N_Y)
        copy = remote(sq_part.at[to], sq_in.at[d - 1], sq_s.at[d - 1], sq_r.at[d - 1], along_tp(d))
        copy.start()
        squares_out.append(copy)

    @pl.loop(1, N_Y - 1)
    def _(s):
        for way in range(2):
            for j in range(SUBS):
                term[way, j] = own_term(group_at(way, s), way, j)
        for h in range(2):
            at = slice(h * half, (h + 1) * half)
            for j in range(SUBS):
                for way in range(2):
                    hop(way, s - 1, j, h).wait_recv()
                    ring[way, s, j, at] = ring[way, s, j, at] + term[way, j, at]
                    hop(way, s, j, h).start()

    for way in range(2):
        for j in range(SUBS):
            term[way, j] = own_term(y, way, j)
    for copy in squares_out:
        copy.wait_recv()
    total = sq_part[y]
    for d in range(1, N_Y):
        total = total + sq_in[d - 1]
    sq_ref[...] = total
    for h in range(2):
        for j in range(SUBS):
            for way in range(2):
                hop(way, N_Y - 2, j, h).wait_recv()
                start = (way * SUBS + j) * width
                for b in range(N_Y):
                    at = slice(h * half + b * few, h * half + (b + 1) * few)
                    to = slice(b * local_rows + h * few, b * local_rows + (h + 1) * few)
                    raw_ref[to, start : start + width] = ring[way, N_Y - 1, j, at] + term[way, j, at]

    for copy in list(first.values()) + sent + squares_out:
        copy.wait_send()

    @pl.loop(0, N_Y - 1)
    def _(s):
        for way in range(2):
            for j in range(SUBS):
                for h in range(2):
                    hop(way, s, j, h).wait_send()


def head(partials, residual, norm_gain, head_weight):
    local_rows, share = residual.shape
    columns = head_weight.shape[1]
    group = N_Y * local_rows
    chips = N_X * N_Z
    width = columns // (2 * SUBS)
    dma = pltpu.SemaphoreType.DMA
    f32 = jnp.float32
    vmem = pl.BlockSpec(memory_space=pltpu.VMEM)
    raw, squares = pl.pallas_call(
        head_kernel,
        out_shape=[
            jax.ShapeDtypeStruct((group, columns), f32),
            jax.ShapeDtypeStruct((8, BLOCK), f32),
        ],
        in_specs=[pl.BlockSpec(memory_space=pl.ANY)] * 4,
        out_specs=[vmem, vmem],
        scratch_shapes=[
            pltpu.VMEM((share, columns), jnp.bfloat16),
            pltpu.VMEM((local_rows, share), f32),
            pltpu.VMEM((local_rows, share), residual.dtype),
            pltpu.VMEM((1, share), f32),
            pltpu.VMEM((2, N_Y - 1, local_rows // 2, share), f32),
            pltpu.VMEM((2, 2, chips, local_rows // 2, share), f32),
            pltpu.VMEM((2 * chips * local_rows, share), jnp.bfloat16),
            pltpu.VMEM((group, BLOCK), f32),
            pltpu.VMEM((N_Y, 8, BLOCK), f32),
            pltpu.VMEM((N_Y - 1, 8, BLOCK), f32),
            pltpu.VMEM((2, N_Y, SUBS, group, width), f32),
            pltpu.VMEM((2, SUBS, group, width), f32),
            dma((4,)),
            dma((2, N_Y - 1)),
            dma((2, N_Y - 1)),
            dma((2, 2 * chips)),
            dma((2, 2 * chips)),
            dma((2, N_Y - 1, SUBS, 2)),
            dma((2, N_Y - 1, SUBS, 2)),
            dma((N_Y - 1,)),
            dma((N_Y - 1,)),
        ],
        compiler_params=pltpu.CompilerParams(
            collective_id=0, has_side_effects=True, vmem_limit_bytes=63 << 20
        ),
    )(partials, residual, norm_gain.reshape(1, share), head_weight)
    return raw, squares[0]


def body(partials, residual, norm_gain, head_weight, owners, allowed, counts):
    raw_logits, sumsq = head(partials, residual, norm_gain, head_weight)
    width = head_weight.shape[0] * lax.axis_size("tp")
    return tail(raw_logits, sumsq, width, owners, allowed, counts)


def solution(mesh):
    placed = (
        P("tp", "vocab", None),
        P("vocab", "tp"),
        P("tp"),
        P("tp", "vocab"),
        P("tp"),
        P("tp", None),
        P("tp"),
    )
    return jax.shard_map(
        body, mesh=mesh, in_specs=placed, out_specs=P(("tp", "vocab"), None, None), check_vma=False
    )
```

```python
import jax
import jax.numpy as jnp
from jax import lax
from jax.experimental import pallas as pl
from jax.experimental.pallas import tpu as pltpu
from jax.sharding import PartitionSpec as P

EPSILON = 1e-05
BLOCK = 128
KMAX = 4


def slot_ranks(owners):
    row_order = jnp.arange(owners.shape[0], dtype=jnp.int32)
    same_owner = (owners[:, None] == owners[None, :]) & (row_order[:, None] < row_order[None, :])
    return jnp.sum(same_owner.astype(jnp.int32), axis=0)


def tail(raw_logits, sumsq, width, owners, allowed, counts):
    vocab_count = lax.axis_size("vocab")
    vocab_index = lax.axis_index("vocab")
    own_rows, columns = raw_logits.shape
    blocks_here = columns // BLOCK
    list_width = allowed.shape[1]
    per_owner = 2 * own_rows // vocab_count
    positions = jnp.arange(list_width, dtype=jnp.int32)

    slot_rank = slot_ranks(owners)
    mine = jnp.where(positions[None, :] < counts[:, None], allowed, -1) - vocab_index * blocks_here
    here = jnp.arange(blocks_here, dtype=jnp.int32)
    present = jnp.any(mine[:, None, :] == here[None, :, None], axis=2).astype(jnp.int32)
    place = jnp.sum(jnp.where(here[:, None] < here[None, :], present[:, :, None], 0), axis=1)
    place = jnp.where(present > 0, place, -1)
    target_row = owners * per_owner + slot_rank
    slots = jnp.arange(vocab_count * per_owner, dtype=jnp.int32)
    to_slot = (target_row[None, :] == slots[:, None]).astype(jnp.float32)

    slot_index = jnp.arange(per_owner, dtype=jnp.int32)[:, None]
    owned_slot = ((owners[None, :] == vocab_index) & (slot_rank[None, :] == slot_index)).astype(jnp.int32)
    slot_lists = jnp.sum(owned_slot[:, :, None] * allowed[None, :, :], axis=1)
    slot_counts = jnp.sum(owned_slot * counts[None, :], axis=1)
    live_entry = positions[None, :] < slot_counts[:, None]
    source = jnp.clip(slot_lists // blocks_here, 0, vocab_count - 1)
    rank = jnp.zeros_like(source)
    for back in range(1, KMAX):
        earlier = jnp.pad(source, ((0, 0), (back, 0)), constant_values=-1)[:, :list_width]
        rank = rank + (earlier == source).astype(jnp.int32)
    table_row = (source * per_owner + slot_index) * (KMAX + 1) + jnp.minimum(rank, KMAX - 1)
    table_row = jnp.where(live_entry, table_row, 0)

    logits = raw_logits * lax.rsqrt(sumsq / width + EPSILON)[:, None]
    row_top = jnp.max(logits, axis=1)
    row_total = jnp.sum(jnp.exp(logits - row_top[:, None]), axis=1)
    picked = []
    for k in range(KMAX):
        chosen = jnp.zeros((own_rows, BLOCK), jnp.float32)
        for b in range(blocks_here):
            block = logits[:, b * BLOCK : (b + 1) * BLOCK]
            chosen = jnp.where((place[:, b] == k)[:, None], block, chosen)
        picked.append(chosen)
    lane = jnp.arange(BLOCK, dtype=jnp.int32)[None, :]
    picked.append(jnp.where(lane == 0, row_top[:, None], jnp.where(lane == 1, row_total[:, None], 0.0)))
    payload = jnp.concatenate(picked, axis=1)
    outgoing = jnp.dot(
        to_slot, payload, precision=lax.Precision.HIGHEST, preferred_element_type=jnp.float32
    ).reshape(vocab_count, per_owner, (KMAX + 1) * BLOCK)
    incoming = lax.all_to_all(outgoing, "vocab", split_axis=0, concat_axis=0, tiled=True)
    tops = incoming[:, :, KMAX * BLOCK]
    totals = incoming[:, :, KMAX * BLOCK + 1]
    big_top = jnp.max(tops, axis=0)
    big_total = jnp.sum(totals * jnp.exp(tops - big_top[None, :]), axis=0)
    shift = big_top + jnp.log(big_total)
    received = incoming.reshape(vocab_count * per_owner * (KMAX + 1), BLOCK)
    gathered = jnp.take(received, table_row, axis=0)
    return jnp.where(live_entry[:, :, None], gathered - shift[:, None, None], 0.0)


N_Y, N_X, N_Z = 8, 4, 8
SUBS = 3
LAG = 3


def head_kernel(
    part_hbm, res_hbm, gain_hbm, w_hbm, raw_ref, sq_ref,
    w, part, res, gain, rs_in, rows, scaled, col, sq_part, sq_in, ring, term,
    in_sem, rs_s, rs_r, ag_s, ag_r, ring_s, ring_r, sq_s, sq_r,
):
    y = lax.axis_index("tp")
    v = lax.axis_index("vocab")
    core = lax.rem(v, 2)
    z = lax.rem(lax.div(v, 2), N_Z)
    x = lax.div(v, 2 * N_Z)
    turn = 1 - 2 * core
    local_rows, share = res.shape
    few = local_rows // 2
    group = N_Y * local_rows
    half = group // 2

    def at_x(q):
        return lax.rem(x - turn * q + N_X, N_X)

    def at_z(p):
        return lax.rem(z - turn * p + N_Z, N_Z)

    def device(p, q, c):
        return (y, (at_x(q) * N_Z + at_z(p)) * 2 + c)

    def along_tp(d):
        return (lax.rem(y + d + N_Y, N_Y), v)

    def columns_of(at):
        return pl.ds(pl.multiple_of(at * share, share), share)

    loads = [
        pltpu.make_async_copy(part_hbm.at[0, :, columns_of(y)], part, in_sem.at[0]),
        pltpu.make_async_copy(res_hbm, res, in_sem.at[1]),
        pltpu.make_async_copy(gain_hbm, gain, in_sem.at[2]),
        pltpu.make_async_copy(w_hbm, w, in_sem.at[3]),
    ]
    for load in loads:
        load.start()

    peers = [along_tp(d) for d in range(1, N_Y)]
    peers += [device(-1, 0, core), device(1, 0, core), device(0, -1, core), device(0, 1, core)]
    peers += [device(0, 0, 1 - core)]
    barrier = pltpu.get_barrier_semaphore()
    for peer in peers:
        pl.semaphore_signal(barrier, inc=1, device_id=peer, device_id_type=pl.DeviceIdType.MESH)
    pl.semaphore_wait(barrier, len(peers))

    def remote(src, dst, send_sem, recv_sem, peer):
        return pltpu.make_async_remote_copy(
            src_ref=src, dst_ref=dst, send_sem=send_sem, recv_sem=recv_sem,
            device_id=peer, device_id_type=pl.DeviceIdType.MESH,
        )

    first = {}
    for h in range(2):
        for d in (4, 1, 7, 2, 6, 3, 5):
            source = part_hbm.at[0, pl.ds(h * few, few), columns_of(lax.rem(y + d, N_Y))]
            copy = remote(
                source, rs_in.at[h, d - 1], rs_s.at[h, d - 1], rs_r.at[h, d - 1], along_tp(d)
            )
            copy.start()
            first[h, d] = copy
    for load in loads[:3]:
        load.wait()
    own = x * N_Z + z

    def mix(h):
        at = slice(h * few, (h + 1) * few)
        mixed = part[at] + res[...].astype(jnp.float32)[at]
        for d in range(1, N_Y):
            first[h, d].wait_recv()
        for d in range(1, N_Y):
            mixed = mixed + rs_in[h, d - 1]
        rows[h, core, own] = mixed

    limits = {"z": (N_Z // 2, N_Z // 2 - 1), "x": (N_X // 2, N_X // 2 - 1)}
    places = [
        (h, p, q)
        for h in range(2)
        for p in range(-limits["z"][1], limits["z"][0] + 1)
        for q in range(-limits["x"][1], limits["x"][0] + 1)
    ]
    ids = {place: i for i, place in enumerate(places)}

    def held(h, p, q):
        return rows.at[h, core, at_x(q) * N_Z + at_z(p)]

    def pass_on(h, p, q, new_p, new_q):
        peer = device(p - new_p, q - new_q, core)
        i = ids[(h, new_p, new_q)]
        remote(held(h, p, q), held(h, p, q), ag_s.at[0, i], ag_r.at[0, i], peer).start()

    def to_sibling(h, p, q):
        i = ids[(h, p, q)]
        remote(
            held(h, p, q), held(h, p, q), ag_s.at[1, i], ag_r.at[1, i], device(0, 0, 1 - core)
        ).start()

    def along_z(h, p, q):
        if 0 <= p < limits["z"][0]:
            pass_on(h, p, q, p + 1, q)
        if -limits["z"][1] < p <= 0:
            pass_on(h, p, q, p - 1, q)

    def along_x(h, p, q):
        if 0 <= q < limits["x"][0]:
            pass_on(h, p, q, p, q + 1)
        if -limits["x"][1] < q <= 0:
            pass_on(h, p, q, p, q - 1)

    def arrived(z_first, h, p, q):
        if z_first:
            if q == 0:
                along_z(h, p, q)
            along_x(h, p, q)
        else:
            if p == 0:
                along_x(h, p, q)
            along_z(h, p, q)
        to_sibling(h, p, q)

    def plan(flip):
        def key(place):
            h, p, q = place
            main, other = (p, q) if h == flip else (q, p)
            return (abs(p) + abs(q) + LAG * h, h, abs(other), main)

        filled = sorted(places, key=key)
        last = max(k for k, place in enumerate(filled) if place[0] == 0)
        return filled[: last + 1], filled[last + 1 :]

    def gather(flip, some):
        for h, p, q in some:
            if (p, q) == (0, 0):
                if h == 1:
                    mix(1)
            else:
                i = ids[(h, p, q)]
                block = held(h, p, q)
                remote(
                    block, block, ag_s.at[0, i], ag_r.at[0, i], device(0, 0, 1 - core)
                ).wait_recv()
            arrived(h == flip, h, p, q)

    def on_each_core(part):
        for flip in range(2):

            @pl.when(core == flip)
            def _():
                gather(flip, plan(flip)[part])

    def wait_siblings(h):
        for place in places:
            if place[0] == h:
                i = ids[place]
                block = rows.at[h, 1 - core, at_x(-place[2]) * N_Z + at_z(-place[1])]
                remote(
                    block, block, ag_s.at[1, i], ag_r.at[1, i], device(0, 0, 1 - core)
                ).wait_recv()

    def prepare(g, h):
        for b in range(N_Y // 2):
            at = lax.div(g * N_Y, 2) + b
            pair = jnp.concatenate([rows[h, 0, at], rows[h, 1, at]], axis=0) * gain[...]
            start = pl.multiple_of(g * group + h * half + b * local_rows, local_rows)
            scaled[pl.ds(start, local_rows), :] = pair.astype(jnp.bfloat16)

    def square(g):
        for b in range(N_Y):
            at = lax.div(g * N_Y, 2) + b // 2
            for h in range(2):
                block = rows[h, b % 2, at]
                squares = jnp.sum(block * block, axis=1, keepdims=True)
                start = b * local_rows + h * few
                col[start : start + few, :] = jnp.broadcast_to(squares, (few, BLOCK))
        sq_part[g] = jnp.transpose(col[...])[:8]

    width = ring.shape[-1]

    def own_term(g, way, j):
        left = scaled[pl.ds(pl.multiple_of(g * group, group), group), :]
        start = (way * SUBS + j) * width
        return jnp.dot(left, w[:, start : start + width], preferred_element_type=jnp.float32)

    def group_at(way, s):
        return lax.rem(y + N_Y - 1 - s, N_Y) if way == 0 else lax.rem(y + 1 + s, N_Y)

    def hop(way, s, j, h):
        at = pl.ds(h * half, half)
        return remote(
            ring.at[way, s, j, at], ring.at[way, s + 1, j, at],
            ring_s.at[way, s, j, h], ring_r.at[way, s, j, h],
            along_tp(1 if way == 0 else -1),
        )

    def begin(h):
        for way in range(2):
            g = group_at(way, 0)
            prepare(g, h)
            left = scaled[pl.ds(pl.multiple_of(g * group + h * half, half), half), :]
            for j in range(SUBS):
                start = (way * SUBS + j) * width
                ring[way, 0, j, h * half : (h + 1) * half] = jnp.dot(
                    left, w[:, start : start + width], preferred_element_type=jnp.float32
                )
                hop(way, 0, j, h).start()

    mix(0)
    on_each_core(0)
    wait_siblings(0)
    loads[3].wait()
    begin(0)
    on_each_core(1)
    wait_siblings(1)
    begin(1)

    @pl.loop(2, N_Y + 1)
    def _(k):
        @pl.when(k != N_Y - 1)
        def _():
            for h in range(2):
                prepare(lax.rem(y + k, N_Y), h)

    @pl.loop(0, N_Y)
    def _(g):
        square(g)

    squares_out = []
    for d in range(1, N_Y):
        to = lax.rem(y + d, N_Y)
        copy = remote(sq_part.at[to], sq_in.at[d - 1], sq_s.at[d - 1], sq_r.at[d - 1], along_tp(d))
        copy.start()
        squares_out.append(copy)

    @pl.loop(1, N_Y - 1)
    def _(s):
        for way in range(2):
            for j in range(SUBS):
                term[way, j] = own_term(group_at(way, s), way, j)
        for h in range(2):
            at = slice(h * half, (h + 1) * half)
            for j in range(SUBS):
                for way in range(2):
                    hop(way, s - 1, j, h).wait_recv()
                    ring[way, s, j, at] = ring[way, s, j, at] + term[way, j, at]
                    hop(way, s, j, h).start()

    for way in range(2):
        for j in range(SUBS):
            term[way, j] = own_term(y, way, j)
    for copy in squares_out:
        copy.wait_recv()
    total = sq_part[y]
    for d in range(1, N_Y):
        total = total + sq_in[d - 1]
    sq_ref[...] = total
    for h in range(2):
        for j in range(SUBS):
            for way in range(2):
                hop(way, N_Y - 2, j, h).wait_recv()
                start = (way * SUBS + j) * width
                for b in range(N_Y):
                    at = slice(h * half + b * few, h * half + (b + 1) * few)
                    to = slice(b * local_rows + h * few, b * local_rows + (h + 1) * few)
                    raw_ref[to, start : start + width] = ring[way, N_Y - 1, j, at] + term[way, j, at]

    for copy in list(first.values()) + squares_out:
        copy.wait_send()
    for place in places:
        i = ids[place]
        block = rows.at[place[0], core, own]
        if place[1:] != (0, 0):
            remote(block, block, ag_s.at[0, i], ag_r.at[0, i], device(0, 0, 1 - core)).wait_send()
        remote(block, block, ag_s.at[1, i], ag_r.at[1, i], device(0, 0, 1 - core)).wait_send()

    @pl.loop(0, N_Y - 1)
    def _(s):
        for way in range(2):
            for j in range(SUBS):
                for h in range(2):
                    hop(way, s, j, h).wait_send()


def head(partials, residual, norm_gain, head_weight):
    local_rows, share = residual.shape
    columns = head_weight.shape[1]
    group = N_Y * local_rows
    chips = N_X * N_Z
    width = columns // (2 * SUBS)
    dma = pltpu.SemaphoreType.DMA
    f32 = jnp.float32
    vmem = pl.BlockSpec(memory_space=pltpu.VMEM)
    raw, squares = pl.pallas_call(
        head_kernel,
        out_shape=[
            jax.ShapeDtypeStruct((group, columns), f32),
            jax.ShapeDtypeStruct((8, BLOCK), f32),
        ],
        in_specs=[pl.BlockSpec(memory_space=pl.ANY)] * 4,
        out_specs=[vmem, vmem],
        scratch_shapes=[
            pltpu.VMEM((share, columns), jnp.bfloat16),
            pltpu.VMEM((local_rows, share), f32),
            pltpu.VMEM((local_rows, share), residual.dtype),
            pltpu.VMEM((1, share), f32),
            pltpu.VMEM((2, N_Y - 1, local_rows // 2, share), f32),
            pltpu.VMEM((2, 2, chips, local_rows // 2, share), f32),
            pltpu.VMEM((2 * chips * local_rows, share), jnp.bfloat16),
            pltpu.VMEM((group, BLOCK), f32),
            pltpu.VMEM((N_Y, 8, BLOCK), f32),
            pltpu.VMEM((N_Y - 1, 8, BLOCK), f32),
            pltpu.VMEM((2, N_Y, SUBS, group, width), f32),
            pltpu.VMEM((2, SUBS, group, width), f32),
            dma((4,)),
            dma((2, N_Y - 1)),
            dma((2, N_Y - 1)),
            dma((2, 2 * chips)),
            dma((2, 2 * chips)),
            dma((2, N_Y - 1, SUBS, 2)),
            dma((2, N_Y - 1, SUBS, 2)),
            dma((N_Y - 1,)),
            dma((N_Y - 1,)),
        ],
        compiler_params=pltpu.CompilerParams(
            collective_id=0, has_side_effects=True, vmem_limit_bytes=63 << 20
        ),
    )(partials, residual, norm_gain.reshape(1, share), head_weight)
    return raw, squares[0]


def body(partials, residual, norm_gain, head_weight, owners, allowed, counts):
    raw_logits, sumsq = head(partials, residual, norm_gain, head_weight)
    width = head_weight.shape[0] * lax.axis_size("tp")
    return tail(raw_logits, sumsq, width, owners, allowed, counts)


def solution(mesh):
    placed = (
        P("tp", "vocab", None),
        P("vocab", "tp"),
        P("tp"),
        P("tp", "vocab"),
        P("tp"),
        P("tp", None),
        P("tp"),
    )
    return jax.shard_map(
        body, mesh=mesh, in_specs=placed, out_specs=P(("tp", "vocab"), None, None), check_vma=False
    )
```

```python
import jax
import jax.numpy as jnp
from jax import lax
from jax.experimental import pallas as pl
from jax.experimental.pallas import tpu as pltpu
from jax.sharding import PartitionSpec as P

EPSILON = 1e-05
BLOCK = 128
KMAX = 4


def slot_ranks(owners):
    row_order = jnp.arange(owners.shape[0], dtype=jnp.int32)
    same_owner = (owners[:, None] == owners[None, :]) & (row_order[:, None] < row_order[None, :])
    return jnp.sum(same_owner.astype(jnp.int32), axis=0)


def tail(raw_logits, sumsq, width, owners, allowed, counts):
    vocab_count = lax.axis_size("vocab")
    vocab_index = lax.axis_index("vocab")
    own_rows, columns = raw_logits.shape
    blocks_here = columns // BLOCK
    list_width = allowed.shape[1]
    per_owner = 2 * own_rows // vocab_count
    positions = jnp.arange(list_width, dtype=jnp.int32)

    slot_rank = slot_ranks(owners)
    mine = jnp.where(positions[None, :] < counts[:, None], allowed, -1) - vocab_index * blocks_here
    here = jnp.arange(blocks_here, dtype=jnp.int32)
    present = jnp.any(mine[:, None, :] == here[None, :, None], axis=2).astype(jnp.int32)
    place = jnp.sum(jnp.where(here[:, None] < here[None, :], present[:, :, None], 0), axis=1)
    place = jnp.where(present > 0, place, -1)
    target_row = owners * per_owner + slot_rank
    slots = jnp.arange(vocab_count * per_owner, dtype=jnp.int32)
    to_slot = (target_row[None, :] == slots[:, None]).astype(jnp.float32)

    slot_index = jnp.arange(per_owner, dtype=jnp.int32)[:, None]
    owned_slot = ((owners[None, :] == vocab_index) & (slot_rank[None, :] == slot_index)).astype(jnp.int32)
    slot_lists = jnp.sum(owned_slot[:, :, None] * allowed[None, :, :], axis=1)
    slot_counts = jnp.sum(owned_slot * counts[None, :], axis=1)
    live_entry = positions[None, :] < slot_counts[:, None]
    source = jnp.clip(slot_lists // blocks_here, 0, vocab_count - 1)
    rank = jnp.zeros_like(source)
    for back in range(1, KMAX):
        earlier = jnp.pad(source, ((0, 0), (back, 0)), constant_values=-1)[:, :list_width]
        rank = rank + (earlier == source).astype(jnp.int32)
    table_row = (source * per_owner + slot_index) * (KMAX + 1) + jnp.minimum(rank, KMAX - 1)
    table_row = jnp.where(live_entry, table_row, 0)

    logits = raw_logits * lax.rsqrt(sumsq / width + EPSILON)[:, None]
    row_top = jnp.max(logits, axis=1)
    row_total = jnp.sum(jnp.exp(logits - row_top[:, None]), axis=1)
    picked = []
    for k in range(KMAX):
        chosen = jnp.zeros((own_rows, BLOCK), jnp.float32)
        for b in range(blocks_here):
            block = logits[:, b * BLOCK : (b + 1) * BLOCK]
            chosen = jnp.where((place[:, b] == k)[:, None], block, chosen)
        picked.append(chosen)
    lane = jnp.arange(BLOCK, dtype=jnp.int32)[None, :]
    picked.append(jnp.where(lane == 0, row_top[:, None], jnp.where(lane == 1, row_total[:, None], 0.0)))
    payload = jnp.concatenate(picked, axis=1)
    outgoing = jnp.dot(
        to_slot, payload, precision=lax.Precision.HIGHEST, preferred_element_type=jnp.float32
    ).reshape(vocab_count, per_owner, (KMAX + 1) * BLOCK)
    incoming = lax.all_to_all(outgoing, "vocab", split_axis=0, concat_axis=0, tiled=True)
    tops = incoming[:, :, KMAX * BLOCK]
    totals = incoming[:, :, KMAX * BLOCK + 1]
    big_top = jnp.max(tops, axis=0)
    big_total = jnp.sum(totals * jnp.exp(tops - big_top[None, :]), axis=0)
    shift = big_top + jnp.log(big_total)
    received = incoming.reshape(vocab_count * per_owner * (KMAX + 1), BLOCK)
    gathered = jnp.take(received, table_row, axis=0)
    return jnp.where(live_entry[:, :, None], gathered - shift[:, None, None], 0.0)


N_Y, N_X, N_Z = 8, 4, 8
SUBS = 3


def head_kernel(
    part_hbm, res_hbm, gain_hbm, w_hbm, raw_ref, sq_ref,
    w, part, res, gain, rs_in, rows, scaled, col, sq_part, sq_in, ring, term,
    in_sem, rs_s, rs_r, ag_s, ag_r, ring_s, ring_r, sq_s, sq_r,
):
    y = lax.axis_index("tp")
    v = lax.axis_index("vocab")
    core = lax.rem(v, 2)
    z = lax.rem(lax.div(v, 2), N_Z)
    x = lax.div(v, 2 * N_Z)
    turn = 1 - 2 * core
    local_rows, share = res.shape
    few = local_rows // 2
    group = N_Y * local_rows
    half = group // 2

    def at_x(q):
        return lax.rem(x - turn * q + N_X, N_X)

    def at_z(p):
        return lax.rem(z - turn * p + N_Z, N_Z)

    def device(p, q, c):
        return (y, (at_x(q) * N_Z + at_z(p)) * 2 + c)

    def along_tp(d):
        return (lax.rem(y + d + N_Y, N_Y), v)

    def columns_of(at):
        return pl.ds(pl.multiple_of(at * share, share), share)

    loads = [
        pltpu.make_async_copy(part_hbm.at[0, :, columns_of(y)], part, in_sem.at[0]),
        pltpu.make_async_copy(res_hbm, res, in_sem.at[1]),
        pltpu.make_async_copy(gain_hbm, gain, in_sem.at[2]),
        pltpu.make_async_copy(w_hbm, w, in_sem.at[3]),
    ]
    for load in loads:
        load.start()

    peers = [along_tp(d) for d in range(1, N_Y)]
    peers += [device(-1, 0, core), device(1, 0, core), device(0, -1, core), device(0, 1, core)]
    peers += [device(0, 0, 1 - core)]
    barrier = pltpu.get_barrier_semaphore()
    for peer in peers:
        pl.semaphore_signal(barrier, inc=1, device_id=peer, device_id_type=pl.DeviceIdType.MESH)
    pl.semaphore_wait(barrier, len(peers))

    def remote(src, dst, send_sem, recv_sem, peer):
        return pltpu.make_async_remote_copy(
            src_ref=src, dst_ref=dst, send_sem=send_sem, recv_sem=recv_sem,
            device_id=peer, device_id_type=pl.DeviceIdType.MESH,
        )

    first = {}
    for h in range(2):
        for d in (4, 1, 7, 2, 6, 3, 5):
            source = part_hbm.at[0, pl.ds(h * few, few), columns_of(lax.rem(y + d, N_Y))]
            copy = remote(
                source, rs_in.at[h, d - 1], rs_s.at[h, d - 1], rs_r.at[h, d - 1], along_tp(d)
            )
            copy.start()
            first[h, d] = copy
    for load in loads[:3]:
        load.wait()
    own = x * N_Z + z

    def mix(h):
        at = slice(h * few, (h + 1) * few)
        mixed = part[at] + res[...].astype(jnp.float32)[at]
        for d in range(1, N_Y):
            first[h, d].wait_recv()
        for d in range(1, N_Y):
            mixed = mixed + rs_in[h, d - 1]
        rows[h, core, own] = mixed

    limits = {"z": (N_Z // 2, N_Z // 2 - 1), "x": (N_X // 2, N_X // 2 - 1)}
    places = [
        (h, p, q)
        for h in range(2)
        for p in range(-limits["z"][1], limits["z"][0] + 1)
        for q in range(-limits["x"][1], limits["x"][0] + 1)
    ]
    ids = {place: i for i, place in enumerate(places)}
    sent = []

    def held(h, p, q):
        return rows.at[h, core, at_x(q) * N_Z + at_z(p)]

    def pass_on(h, p, q, new_p, new_q):
        peer = device(p - new_p, q - new_q, core)
        i = ids[(h, new_p, new_q)]
        copy = remote(held(h, p, q), held(h, p, q), ag_s.at[0, i], ag_r.at[0, i], peer)
        copy.start()
        sent.append(copy)

    def to_sibling(h, p, q):
        i = ids[(h, p, q)]
        copy = remote(
            held(h, p, q), held(h, p, q), ag_s.at[1, i], ag_r.at[1, i], device(0, 0, 1 - core)
        )
        copy.start()
        sent.append(copy)

    def along_z(h, p, q):
        if 0 <= p < limits["z"][0]:
            pass_on(h, p, q, p + 1, q)
        if -limits["z"][1] < p <= 0:
            pass_on(h, p, q, p - 1, q)

    def along_x(h, p, q):
        if 0 <= q < limits["x"][0]:
            pass_on(h, p, q, p, q + 1)
        if -limits["x"][1] < q <= 0:
            pass_on(h, p, q, p, q - 1)

    def arrived(h, p, q):
        if h == 0:
            if q == 0:
                along_z(h, p, q)
            along_x(h, p, q)
        else:
            if p == 0:
                along_x(h, p, q)
            along_z(h, p, q)
        to_sibling(h, p, q)

    def order(place):
        h, p, q = place
        main, other = (p, q) if h == 0 else (q, p)
        return (abs(p) + abs(q) + 3 * h, abs(other), h, main)

    def wait_siblings(h):
        for _, p, q in sorted((place for place in places if place[0] == h), key=order):
            i = ids[(h, p, q)]
            block = rows.at[h, 1 - core, at_x(-q) * N_Z + at_z(-p)]
            remote(block, block, ag_s.at[1, i], ag_r.at[1, i], device(0, 0, 1 - core)).wait_recv()

    def prepare(g, h):
        for b in range(N_Y // 2):
            at = lax.div(g * N_Y, 2) + b
            pair = jnp.concatenate([rows[h, 0, at], rows[h, 1, at]], axis=0) * gain[...]
            start = pl.multiple_of(g * group + h * half + b * local_rows, local_rows)
            scaled[pl.ds(start, local_rows), :] = pair.astype(jnp.bfloat16)

    def square(g):
        for b in range(N_Y):
            at = lax.div(g * N_Y, 2) + b // 2
            for h in range(2):
                block = rows[h, b % 2, at]
                squares = jnp.sum(block * block, axis=1, keepdims=True)
                start = b * local_rows + h * few
                col[start : start + few, :] = jnp.broadcast_to(squares, (few, BLOCK))
        sq_part[g] = jnp.transpose(col[...])[:8]

    width = ring.shape[-1]

    def own_term(g, way, j, h):
        left = scaled[pl.ds(pl.multiple_of(g * group + h * half, half), half), :]
        start = (way * SUBS + j) * width
        return jnp.dot(left, w[:, start : start + width], preferred_element_type=jnp.float32)

    def group_at(way, s):
        return lax.rem(y + N_Y - 1 - s, N_Y) if way == 0 else lax.rem(y + 1 + s, N_Y)

    def hop(way, s, j, h):
        at = pl.ds(h * half, half)
        return remote(
            ring.at[way, s, j, at], ring.at[way, s + 1, j, at],
            ring_s.at[way, s, j, h], ring_r.at[way, s, j, h],
            along_tp(1 if way == 0 else -1),
        )

    def begin(h):
        for way in range(2):
            g = group_at(way, 0)
            prepare(g, h)
            for j in range(SUBS):
                ring[way, 0, j, h * half : (h + 1) * half] = own_term(g, way, j, h)
                hop(way, 0, j, h).start()

    mix(0)
    waiting = sorted(places, key=order)
    for place in waiting:
        h, p, q = place
        if (p, q) == (0, 0):
            if h == 1:
                mix(1)
        else:
            i = ids[place]
            block = held(h, p, q)
            remote(block, block, ag_s.at[0, i], ag_r.at[0, i], device(0, 0, 1 - core)).wait_recv()
        arrived(h, p, q)
        if place == [other for other in waiting if other[0] == 0][-1]:
            wait_siblings(0)
            loads[3].wait()
            begin(0)
    def step(s, h, fresh):
        at = slice(h * half, (h + 1) * half)
        if fresh:
            for way in range(2):
                prepare(group_at(way, s), h)
        for way in range(2):
            for j in range(SUBS):
                term[way, j, at] = own_term(group_at(way, s), way, j, h)
        for j in range(SUBS):
            for way in range(2):
                hop(way, s - 1, j, h).wait_recv()
                ring[way, s, j, at] = ring[way, s, j, at] + term[way, j, at]
                hop(way, s, j, h).start()

    step(1, 0, True)
    wait_siblings(1)
    begin(1)
    step(2, 0, True)

    @pl.loop(1, N_Y // 2)
    def _(s):
        step(s, 1, True)
        step(s + 2, 0, True)
        square(2 * s - 2)
        square(2 * s - 1)

    for h in range(2):
        prepare(y, h)
    square(N_Y - 2)
    square(N_Y - 1)

    squares_out = []
    for d in range(1, N_Y):
        to = lax.rem(y + d, N_Y)
        copy = remote(sq_part.at[to], sq_in.at[d - 1], sq_s.at[d - 1], sq_r.at[d - 1], along_tp(d))
        copy.start()
        squares_out.append(copy)

    @pl.loop(N_Y // 2, N_Y - 1)
    def _(s):
        step(s, 1, False)

        @pl.when(s + 2 < N_Y - 1)
        def _():
            step(s + 2, 0, False)

    for h in range(2):
        for way in range(2):
            for j in range(SUBS):
                term[way, j, h * half : (h + 1) * half] = own_term(y, way, j, h)
    for copy in squares_out:
        copy.wait_recv()
    total = sq_part[y]
    for d in range(1, N_Y):
        total = total + sq_in[d - 1]
    sq_ref[...] = total
    for h in range(2):
        for j in range(SUBS):
            for way in range(2):
                hop(way, N_Y - 2, j, h).wait_recv()
                start = (way * SUBS + j) * width
                for b in range(N_Y):
                    at = slice(h * half + b * few, h * half + (b + 1) * few)
                    to = slice(b * local_rows + h * few, b * local_rows + (h + 1) * few)
                    raw_ref[to, start : start + width] = ring[way, N_Y - 1, j, at] + term[way, j, at]

    for copy in list(first.values()) + sent + squares_out:
        copy.wait_send()

    @pl.loop(0, N_Y - 1)
    def _(s):
        for way in range(2):
            for j in range(SUBS):
                for h in range(2):
                    hop(way, s, j, h).wait_send()


def head(partials, residual, norm_gain, head_weight):
    local_rows, share = residual.shape
    columns = head_weight.shape[1]
    group = N_Y * local_rows
    chips = N_X * N_Z
    width = columns // (2 * SUBS)
    dma = pltpu.SemaphoreType.DMA
    f32 = jnp.float32
    vmem = pl.BlockSpec(memory_space=pltpu.VMEM)
    raw, squares = pl.pallas_call(
        head_kernel,
        out_shape=[
            jax.ShapeDtypeStruct((group, columns), f32),
            jax.ShapeDtypeStruct((8, BLOCK), f32),
        ],
        in_specs=[pl.BlockSpec(memory_space=pl.ANY)] * 4,
        out_specs=[vmem, vmem],
        scratch_shapes=[
            pltpu.VMEM((share, columns), jnp.bfloat16),
            pltpu.VMEM((local_rows, share), f32),
            pltpu.VMEM((local_rows, share), residual.dtype),
            pltpu.VMEM((1, share), f32),
            pltpu.VMEM((2, N_Y - 1, local_rows // 2, share), f32),
            pltpu.VMEM((2, 2, chips, local_rows // 2, share), f32),
            pltpu.VMEM((2 * chips * local_rows, share), jnp.bfloat16),
            pltpu.VMEM((group, BLOCK), f32),
            pltpu.VMEM((N_Y, 8, BLOCK), f32),
            pltpu.VMEM((N_Y - 1, 8, BLOCK), f32),
            pltpu.VMEM((2, N_Y, SUBS, group, width), f32),
            pltpu.VMEM((2, SUBS, group, width), f32),
            dma((4,)),
            dma((2, N_Y - 1)),
            dma((2, N_Y - 1)),
            dma((2, 2 * chips)),
            dma((2, 2 * chips)),
            dma((2, N_Y - 1, SUBS, 2)),
            dma((2, N_Y - 1, SUBS, 2)),
            dma((N_Y - 1,)),
            dma((N_Y - 1,)),
        ],
        compiler_params=pltpu.CompilerParams(
            collective_id=0, has_side_effects=True, vmem_limit_bytes=63 << 20
        ),
    )(partials, residual, norm_gain.reshape(1, share), head_weight)
    return raw, squares[0]


def body(partials, residual, norm_gain, head_weight, owners, allowed, counts):
    raw_logits, sumsq = head(partials, residual, norm_gain, head_weight)
    width = head_weight.shape[0] * lax.axis_size("tp")
    return tail(raw_logits, sumsq, width, owners, allowed, counts)


def solution(mesh):
    placed = (
        P("tp", "vocab", None),
        P("vocab", "tp"),
        P("tp"),
        P("tp", "vocab"),
        P("tp"),
        P("tp", None),
        P("tp"),
    )
    return jax.shard_map(
        body, mesh=mesh, in_specs=placed, out_specs=P(("tp", "vocab"), None, None), check_vma=False
    )
```
